512 devices in a mesh: ctx: 64 (over y, z), head: 8 (over x, core).
Axes of the slice: x: 4, y: 4, z: 16, core: 2. Of those that a mesh axis runs over, the one named last changes fastest.
Arguments:
- queries: bfloat16 [32768, 4096], P(('ctx', 'head')), may hold values from -12 to 12
- keys: bfloat16 [32768, 1024], P(('ctx', 'head')), may hold values from -12 to 12
- values: bfloat16 [32768, 1024], P(('ctx', 'head')), may hold values from -6 to 6
- doc_lengths: int32 [16], replicated, may hold values from 1 to 4096, 32768 in all
- piece_owner: int32 [64, 64], P('ctx'), may hold values from 0 to 63, each once within a row
Outputs:
- owned: bfloat16 [32768, 4096], P('ctx', 'head')
The draws below stay inside these ranges and needn't reach their ends.
Inputs may be any that keep to these rules, and one draw needn't show every extreme that they name: Each row of piece_owner is a permutation of 0 .. 63. doc_lengths sum to 32768, and the largest equals 4096.
All inputs are finite; a program needn't handle non-finite values.
Results may differ from the reference program's by a relative error of at most 0.0033.
Values may be sent and summed in bfloat16 or wider, within the bound.
A program may use at most 64 MiB of HBM per device.

```python
import math
import jax
import jax.numpy as jnp
import numpy as np
from jax import lax

HD = 128
KVH = 8
QPK = 4
QH = 32
TOK_DEV = 512
MOST = 4096
SEQ = 32768
NDOC = 16
REACH = 8
PIECE = 8
N_CTX = 64


def draw_queries(key, part):
    drawn = 1.5 * jnp.clip(jax.random.normal(jax.random.fold_in(key, 11), (SEQ, QH * HD)), -6.0, 6.0)
    return drawn.astype(jnp.bfloat16)


def draw_keys(key, part):
    drawn = 1.33 * jnp.clip(jax.random.normal(jax.random.fold_in(key, 23), (SEQ, KVH * HD)), -6.0, 6.0)
    return drawn.astype(jnp.bfloat16)


def block_levels(stream_key, shape, shards, low, high):
    def one(position, shards_of):
        steps = jax.random.uniform(jax.random.fold_in(jax.random.fold_in(stream_key, 6), position), (shards_of,), jnp.float32, low / len(shards), high / len(shards))
        return jnp.repeat(jnp.exp(steps), shape[position] // shards_of).reshape((-1,) + (1,) * (len(shape) - position - 1))

    gain = one(*shards[0])
    for cut in shards[1:]:
        gain = gain * one(*cut)
    return gain


def profile(number_of, total, reach, slope):
    portions = [(1 << 20) // math.isqrt(grade ** slope) + 1 for grade in range(2, number_of + 1)]
    rest, holding = total - reach - (number_of - 1), [1] * (number_of - 1)
    while rest > 0:
        candidates = [i for i in range(number_of - 1) if holding[i] < reach]
        whole, budget = sum([portions[i] for i in candidates]), rest
        for i in candidates:
            extra = min(reach - holding[i], max(1, budget * portions[i] // whole), rest)
            holding[i] = holding[i] + extra
            rest = rest - extra
    return np.array([reach] + holding)


def uneven_parts(own_key, number_of, total, reach, skew):
    if number_of == 2:
        one = jax.random.randint(own_key, (), max(1, total - reach), min(reach, total - 1) + 1)
        return jnp.stack([one, total - one])
    lengths = jnp.asarray(profile(number_of, total, reach, skew), jnp.int32)
    couples = (number_of - 1) // 2
    donor, receiver = lengths[1:1 + 2 * couples:2], lengths[2:2 + 2 * couples:2]
    slack = jnp.minimum(donor - 1, reach - receiver)
    passed = jax.random.randint(jax.random.fold_in(own_key, 1), (couples,), 0, 1 << 20) % (slack + 1)
    lengths = lengths.at[1:1 + 2 * couples:2].set(donor - passed).at[2:2 + 2 * couples:2].set(receiver + passed)
    return lengths[jax.random.permutation(jax.random.fold_in(own_key, 2), number_of)]


def normal_values(own_key, dims, scale, limit, cuts=(), held_as=jnp.bfloat16):
    gain = block_levels(own_key, dims, cuts, -0.22, 0.18) if cuts else 1.0
    values = jax.random.normal(own_key, dims, jnp.float32) * scale * gain
    return jnp.minimum(jnp.maximum(values, -limit), limit).astype(held_as)


def setup_inputs(seed: int = 0) -> dict:
    arg_keys = jax.random.split(jax.random.key(seed), 6)
    return {
        "queries": draw_queries(jax.random.fold_in(arg_keys[5], 71), 0),
        "keys": draw_keys(jax.random.fold_in(arg_keys[5], 71), 0),
        "values": normal_values(arg_keys[2], (SEQ, KVH * HD), 1.0, 6.0, ((0, 512),)),
        "doc_lengths": uneven_parts(arg_keys[3], NDOC, SEQ, MOST, 2).astype(jnp.int32),
        "piece_owner": jax.vmap(lambda own: jax.random.permutation(own, N_CTX))(jax.random.split(arg_keys[4], N_CTX)).reshape((N_CTX, N_CTX)).astype(jnp.int32),
    }


masked_score = -1e+30

def doc_index(positions, doc_lengths):
    doc_ends = jnp.cumsum(doc_lengths).astype(jnp.int32)
    return lax.optimization_barrier(jnp.sum((positions[:, None] >= doc_ends[None, :]).astype(jnp.int32), axis=1)).astype(jnp.int32)

def reference(queries, keys, values, doc_lengths, piece_owner):
    window_rows = (REACH + 1) * TOK_DEV
    pad_rows = REACH * TOK_DEV
    score_scale = 1.0 / math.sqrt(HD)
    positions = jnp.arange(SEQ, dtype=jnp.int32)
    doc_ids = doc_index(positions, doc_lengths)
    keys_padded = jnp.concatenate([jnp.zeros((pad_rows, KVH * HD), keys.dtype), keys], axis=0)
    values_padded = jnp.concatenate([jnp.zeros((pad_rows, KVH * HD), values.dtype), values], axis=0)
    ids_padded = jnp.concatenate([jnp.full((pad_rows,), -1, jnp.int32), doc_ids], axis=0)

    def one_block(block_index):
        block_start = (block_index * TOK_DEV).astype(jnp.int32)
        query_block = lax.dynamic_slice_in_dim(queries, block_start, TOK_DEV, 0).astype(jnp.float32).reshape(TOK_DEV, KVH, QPK, HD)
        key_block = lax.dynamic_slice_in_dim(keys_padded, block_start, window_rows, 0).astype(jnp.float32).reshape(window_rows, KVH, HD)
        value_block = lax.dynamic_slice_in_dim(values_padded, block_start, window_rows, 0).astype(jnp.float32).reshape(window_rows, KVH, HD)
        query_position = block_start + jnp.arange(TOK_DEV, dtype=jnp.int32)
        key_position = block_start - pad_rows + jnp.arange(window_rows, dtype=jnp.int32)
        query_ids = lax.dynamic_slice_in_dim(doc_ids, block_start, TOK_DEV, 0)
        key_ids = lax.dynamic_slice_in_dim(ids_padded, block_start, window_rows, 0)
        live_pairs = (key_position[None, :] >= 0) & (key_position[None, :] <= query_position[:, None]) & (key_ids[None, :] == query_ids[:, None])
        live_mask = live_pairs[:, None, None, :]
        scores = jnp.einsum('qgjd,kgd->qgjk', query_block, key_block) * score_scale
        scores = jnp.where(live_mask, scores, masked_score)
        row_top = lax.optimization_barrier(jnp.max(scores, axis=-1, keepdims=True))
        weights = jnp.where(live_mask, jnp.exp(scores - row_top), 0.0)
        row_total = lax.optimization_barrier(jnp.sum(weights, axis=-1))
        rounded = lax.optimization_barrier(weights.astype(jnp.bfloat16)).astype(jnp.float32)
        weighted = jnp.einsum('qgjk,kgd->qgjd', rounded, value_block)
        result = weighted / row_total[..., None]
        return result.reshape(TOK_DEV, QH * HD).astype(jnp.bfloat16)
    attended = lax.map(one_block, jnp.arange(N_CTX, dtype=jnp.int32)).reshape(SEQ, QH * HD)
    source_rows = jnp.broadcast_to(jnp.arange(N_CTX, dtype=jnp.int32)[:, None], (N_CTX, N_CTX))
    piece_cols = jnp.broadcast_to(jnp.arange(N_CTX, dtype=jnp.int32)[None, :], (N_CTX, N_CTX))
    inverse = jnp.zeros((N_CTX, N_CTX), jnp.int32).at[source_rows, piece_owner].set(piece_cols)
    pieces = attended.reshape(N_CTX, N_CTX, PIECE, QH * HD)
    taken = jnp.take_along_axis(pieces, inverse[:, :, None, None], axis=1)
    owned = jnp.transpose(taken, (1, 0, 2, 3)).reshape(SEQ, QH * HD)
    return owned
```

```python
import math

import jax
import jax.numpy as jnp
from jax import lax
from jax.experimental import pallas as pl
from jax.experimental.pallas import tpu as pltpu
from jax.sharding import PartitionSpec as P

HD = 128
QPK = 4
MOST = 4096
NDOC = 16
Y = 4
Z = 16
CTX = Y * Z
HEADS = 8
TOK = 512
OWN = TOK // HEADS
REACH = MOST // TOK
PIECE = TOK // CTX
ROWS = 256
CHUNKS = 4
HALF = TOK // 2
MESH = pl.DeviceIdType.MESH
masked_score = -1e30
FACTOR = math.log2(math.e) / math.sqrt(HD)


def wide(x, n):
    return jnp.concatenate([x] * n, axis=1)


def kernel(
    q_ref,
    k_ref,
    v_ref,
    docs,
    owner,
    out,
    qbuf,
    kv,
    first,
    top,
    acc,
    att,
    ordered,
    q_send,
    q_recv,
    kv_send,
    kv_recv,
    ring_send,
    ring_recv,
    out_send,
    out_recv,
    local,
):
    ctx = lax.axis_index("ctx")
    head = lax.axis_index("head")
    cy, cz = ctx // Z, ctx % Z

    def target_of(o):
        dy = 3 - o % Y
        k = o // Y
        size = 8 - (k + 1) // 2
        dz = jnp.where(k % 2 == 1, size, Z - size)
        return ((cy + dy) % Y) * Z + (cz + dz) % Z

    barrier = pltpu.get_barrier_semaphore()
    for o in range(1, HEADS):
        pl.semaphore_signal(
            barrier, inc=1, device_id=(ctx, (head + o) % HEADS), device_id_type=MESH
        )

    def greet(o, c):
        pl.semaphore_signal(barrier, inc=1, device_id=(target_of(o), head), device_id_type=MESH)
        return c

    lax.fori_loop(0, CTX - 1, greet, 0)
    pl.semaphore_wait(barrier, HEADS - 1 + CTX - 1)

    def cols(h, n):
        return pl.ds(pl.multiple_of(h * n, n), n)

    def rows_of(h):
        return pl.ds(pl.multiple_of(h * OWN, OWN), OWN)

    sides = (k_ref, v_ref)

    def kv_copy(o, side, source, target):
        return pltpu.make_async_remote_copy(
            src_ref=sides[side].at[:, cols(target, HD)],
            dst_ref=kv.at[0, side, rows_of(source)],
            send_sem=kv_send.at[o, side],
            recv_sem=kv_recv.at[o, side],
            device_id=(ctx, target),
            device_id_type=MESH,
        )

    def q_copy(o, source, target):
        return pltpu.make_async_remote_copy(
            src_ref=q_ref.at[:, cols(target, QPK * HD)],
            dst_ref=qbuf.at[rows_of(source)],
            send_sem=q_send.at[o],
            recv_sem=q_recv.at[o],
            device_id=(ctx, target),
            device_id_type=MESH,
        )

    for side in range(2):
        for o in range(1, HEADS):
            kv_copy(o, side, head, (head + o) % HEADS).start()
    for o in range(1, HEADS):
        q_copy(o, head, (head + o) % HEADS).start()
    own = [
        pltpu.make_async_copy(
            sides[side].at[:, cols(head, HD)], kv.at[0, side, rows_of(head)], local.at[side]
        )
        for side in range(2)
    ]
    own.append(
        pltpu.make_async_copy(
            q_ref.at[:, cols(head, QPK * HD)], qbuf.at[rows_of(head)], local.at[2]
        )
    )
    for copy in own:
        copy.start()

    following = (ctx + 1) % CTX

    def ring_copy(d, chunk):
        side, part = chunk // 2, chunk % 2
        return pltpu.make_async_remote_copy(
            src_ref=kv.at[d - 1, side, pl.ds(part * HALF, HALF)],
            dst_ref=kv.at[d, side, pl.ds(part * HALF, HALF)],
            send_sem=ring_send.at[d - 1, chunk],
            recv_sem=ring_recv.at[d - 1, chunk],
            device_id=(following, head),
            device_id_type=MESH,
        )

    for side in range(2):
        own[side].wait()
        for o in range(1, HEADS):
            kv_copy(o, side, (head - o) % HEADS, head).wait_recv()
        for part in range(2):
            ring_copy(1, side * 2 + part).start()

    place = ctx * TOK + lax.broadcasted_iota(jnp.int32, (TOK, HD), 0)
    begin = jnp.zeros((TOK, HD), jnp.int32)
    end = jnp.int32(0)
    for i in range(NDOC):
        end = end + docs[i]
        begin = jnp.where(place >= end, end, begin)
    first[...] = begin

    own[2].wait()
    for o in range(1, HEADS):
        q_copy(o, (head - o) % HEADS, head).wait_recv()

    def attend(d, diagonal):
        tiles = TOK // ROWS
        k_block = kv[d, 0]
        v_block = jnp.concatenate([kv[d, 1], jnp.ones((TOK, HD), jnp.bfloat16)], axis=1)
        base = (ctx - d) * TOK
        column = lax.broadcasted_iota(jnp.int32, (ROWS, TOK), 1)
        for j in range(QPK):

            def one(t, c):
                rows = pl.ds(pl.multiple_of(t * ROWS, ROWS), ROWS)
                q = qbuf[rows, j * HD : (j + 1) * HD]
                s = lax.dot_general(
                    q, k_block, (((1,), (1,)), ((), ())), preferred_element_type=jnp.float32
                )
                live = column >= wide(first[rows] - base, TOK // HD)
                if diagonal:
                    row = t * ROWS + lax.broadcasted_iota(jnp.int32, (ROWS, TOK), 0)
                    live = live & (column <= row)
                s = jnp.where(live, s, masked_score)
                peak = jnp.broadcast_to(jnp.max(s, axis=1, keepdims=True), (ROWS, HD))
                if diagonal:
                    new = peak
                else:
                    old = top[j, rows]
                    new = jnp.maximum(old, peak)
                p = jnp.exp2((s - wide(new, TOK // HD)) * FACTOR).astype(jnp.bfloat16)
                pv = jnp.dot(p, v_block, preferred_element_type=jnp.float32)
                if not diagonal:
                    keep = jnp.exp2((old - new) * FACTOR)
                    pv = pv + acc[j, rows] * wide(keep, 2)
                acc[j, rows] = pv
                top[j, rows] = new
                return c

            lax.fori_loop(0, tiles, one, 0)

    attend(0, True)

    def step(d, c):
        for chunk in range(CHUNKS):
            ring_copy(d, chunk).wait_recv()

            @pl.when(d < REACH)
            def _():
                ring_copy(d + 1, chunk).start()

        attend(d, False)
        return c

    lax.fori_loop(1, REACH + 1, step, 0)

    for j in range(QPK):
        att[:, j * HD : (j + 1) * HD] = (acc[j, :, :HD] / acc[j, :, HD:]).astype(jnp.bfloat16)
    spread = (
        lax.broadcasted_iota(jnp.int32, (CTX, TOK), 1) // PIECE
        == lax.broadcasted_iota(jnp.int32, (CTX, TOK), 0)
    ).astype(jnp.bfloat16)
    owners = jnp.broadcast_to(owner[...].astype(jnp.float32), (8, CTX)).astype(jnp.bfloat16)
    owner_of = jnp.dot(owners, spread, preferred_element_type=jnp.float32).astype(jnp.int32)
    column = lax.broadcasted_iota(jnp.int32, (8, TOK), 1)
    goal = (owner_of * PIECE + column % PIECE)[:1]
    swap = (lax.broadcasted_iota(jnp.int32, (TOK, TOK), 0) == goal).astype(jnp.bfloat16)
    moved = jnp.dot(swap, att[...], preferred_element_type=jnp.float32)
    ordered[...] = moved.reshape(CTX, PIECE, QPK * HD).astype(jnp.bfloat16)

    def deliver(o, c):
        target = target_of(o)
        pltpu.make_async_remote_copy(
            src_ref=ordered.at[target],
            dst_ref=out.at[ctx],
            send_sem=out_send,
            recv_sem=out_recv,
            device_id=(target, head),
            device_id_type=MESH,
        ).start()
        return c

    lax.fori_loop(0, CTX - 1, deliver, 0)
    mine = pltpu.make_async_copy(ordered.at[ctx], out.at[ctx], local.at[3])
    mine.start()

    for side in range(2):
        for o in range(1, HEADS):
            kv_copy(o, side, head, (head + o) % HEADS).wait_send()
    for o in range(1, HEADS):
        q_copy(o, head, (head + o) % HEADS).wait_send()

    def drain(d, c):
        for chunk in range(CHUNKS):
            ring_copy(d, chunk).wait_send()
        return c

    lax.fori_loop(1, REACH + 1, drain, 0)
    mine.wait()
    rest = pltpu.make_async_remote_copy(
        src_ref=ordered.at[pl.ds(0, CTX - 1)],
        dst_ref=out.at[pl.ds(0, CTX - 1)],
        send_sem=out_send,
        recv_sem=out_recv,
        device_id=(following, head),
        device_id_type=MESH,
    )
    rest.wait_send()
    rest.wait_recv()


def per_device(queries, keys, values, doc_lengths, piece_owner):
    whole = pl.BlockSpec(memory_space=pl.ANY)
    owned = pl.pallas_call(
        kernel,
        out_shape=jax.ShapeDtypeStruct((CTX, PIECE, QPK * HD), jnp.bfloat16),
        in_specs=[
            whole,
            whole,
            whole,
            pl.BlockSpec(memory_space=pltpu.SMEM),
            pl.BlockSpec(memory_space=pltpu.VMEM),
        ],
        out_specs=whole,
        scratch_shapes=[
            pltpu.VMEM((TOK, QPK * HD), jnp.bfloat16),
            pltpu.VMEM((REACH + 1, 2, TOK, HD), jnp.bfloat16),
            pltpu.VMEM((TOK, HD), jnp.int32),
            pltpu.VMEM((QPK, TOK, HD), jnp.float32),
            pltpu.VMEM((QPK, TOK, 2 * HD), jnp.float32),
            pltpu.VMEM((TOK, QPK * HD), jnp.bfloat16),
            pltpu.VMEM((CTX, PIECE, QPK * HD), jnp.bfloat16),
            pltpu.SemaphoreType.DMA((HEADS,)),
            pltpu.SemaphoreType.DMA((HEADS,)),
            pltpu.SemaphoreType.DMA((HEADS, 2)),
            pltpu.SemaphoreType.DMA((HEADS, 2)),
            pltpu.SemaphoreType.DMA((REACH, CHUNKS)),
            pltpu.SemaphoreType.DMA((REACH, CHUNKS)),
            pltpu.SemaphoreType.DMA,
            pltpu.SemaphoreType.DMA,
            pltpu.SemaphoreType.DMA((4,)),
        ],
        compiler_params=pltpu.CompilerParams(
            collective_id=0, has_side_effects=True, vmem_limit_bytes=32 * 1024 * 1024
        ),
    )(queries, keys, values, doc_lengths, piece_owner)
    return owned.reshape(TOK, QPK * HD)


def solution(mesh):
    return jax.shard_map(
        per_device,
        mesh=mesh,
        in_specs=(
            P(("ctx", "head"), None),
            P(("ctx", "head"), None),
            P(("ctx", "head"), None),
            P(),
            P("ctx", None),
        ),
        out_specs=P("ctx", "head"),
        check_vma=False,
    )
```

```python
import math

import jax
import jax.numpy as jnp
from jax import lax
from jax.experimental import pallas as pl
from jax.experimental.pallas import tpu as pltpu
from jax.sharding import PartitionSpec as P

HD = 128
QPK = 4
MOST = 4096
NDOC = 16
Y = 4
Z = 16
CTX = Y * Z
HEADS = 8
TOK = 512
OWN = TOK // HEADS
REACH = MOST // TOK
PIECE = TOK // CTX
ROWS = 256
EXTRA = 16
WIDE = 256
CHUNK = 64
CHUNKS = TOK // CHUNK
MESH = pl.DeviceIdType.MESH
dead_score = -1e30
FACTOR = math.log2(math.e) / math.sqrt(HD)


def kernel(
    q_ref,
    k_ref,
    v_ref,
    docs_ref,
    owner_ref,
    out,
    docs,
    owner,
    qbuf,
    kv,
    qdoc,
    qt,
    kdoc,
    top,
    acc,
    att,
    swap,
    ordered,
    q_send,
    q_recv,
    kv_send,
    kv_recv,
    ring_send,
    ring_recv,
    out_send,
    out_recv,
    local,
    from_left,
    from_right,
):
    ctx = lax.axis_index("ctx")
    head = lax.axis_index("head")
    cy, cz = lax.div(ctx, Z), lax.rem(ctx, Z)

    def at(dy, dz):
        return lax.rem(cy + dy, Y) * Z + lax.rem(cz + dz, Z)

    tables = [
        pltpu.make_async_copy(docs_ref, docs, local.at[4]),
        pltpu.make_async_copy(owner_ref, owner, local.at[5]),
    ]
    for copy in tables:
        copy.start()
    following, previous = lax.rem(ctx + 1, CTX), lax.rem(ctx + CTX - 1, CTX)
    left, right = at(0, Z - 1), at(0, 1)
    barrier = pltpu.get_barrier_semaphore()

    def signal(sem, where):
        pl.semaphore_signal(sem, inc=1, device_id=where, device_id_type=MESH)

    for o in range(1, HEADS):
        signal(barrier, (ctx, lax.rem(head + o, HEADS)))
    near = (following, previous, left, right, at(1, 0), at(2, 0), at(3, 0))
    for place in near:
        signal(barrier, (place, head))
    pl.semaphore_wait(barrier, HEADS - 1 + len(near))

    def cols(h, n):
        return pl.ds(pl.multiple_of(h * n, n), n)

    def rows_of(h):
        return pl.ds(pl.multiple_of(h * OWN, OWN), OWN)

    sides = (k_ref, v_ref)

    def kv_copy(o, side, source, target):
        return pltpu.make_async_remote_copy(
            src_ref=sides[side].at[:, cols(target, HD)],
            dst_ref=kv.at[0, side, rows_of(source)],
            send_sem=kv_send.at[o, side],
            recv_sem=kv_recv.at[o, side],
            device_id=(ctx, target),
            device_id_type=MESH,
        )

    def q_copy(o, source, target):
        return pltpu.make_async_remote_copy(
            src_ref=q_ref.at[:, cols(target, QPK * HD)],
            dst_ref=qbuf.at[rows_of(source)],
            send_sem=q_send.at[o],
            recv_sem=q_recv.at[o],
            device_id=(ctx, target),
            device_id_type=MESH,
        )

    def peer(o):
        return lax.rem(head + o, HEADS)

    def source(o):
        return lax.rem(head + HEADS - o, HEADS)

    for side in range(2):
        for o in range(1, HEADS):
            kv_copy(o, side, head, peer(o)).start()
    for o in range(1, HEADS):
        q_copy(o, head, peer(o)).start()
    own = [
        pltpu.make_async_copy(
            sides[side].at[:, cols(head, HD)], kv.at[0, side, rows_of(head)], local.at[side]
        )
        for side in range(2)
    ]
    own.append(
        pltpu.make_async_copy(
            q_ref.at[:, cols(head, QPK * HD)], qbuf.at[rows_of(head)], local.at[2]
        )
    )
    for copy in own:
        copy.start()

    def greet():
        signal(from_left, (right, head))
        signal(from_right, (left, head))
        pl.semaphore_wait(from_left, 1)
        pl.semaphore_wait(from_right, 1)

    def ring_copy(n):
        d, begin = lax.div(n, CHUNKS), pl.multiple_of(lax.rem(n, CHUNKS) * CHUNK, CHUNK)
        return pltpu.make_async_remote_copy(
            src_ref=kv.at[d, :, pl.ds(begin, CHUNK)],
            dst_ref=kv.at[d + 1, :, pl.ds(begin, CHUNK)],
            send_sem=ring_send.at[n],
            recv_sem=ring_recv.at[n],
            device_id=(following, head),
            device_id_type=MESH,
        )

    for side in range(2):
        own[side].wait()
        for o in range(1, HEADS):
            kv_copy(o, side, source(o), head).wait_recv()
    for n in range(CHUNKS):
        ring_copy(n).start()

    for copy in tables:
        copy.wait()
    lane = lax.broadcasted_iota(jnp.int32, (TOK, HD), 1)
    row = lax.broadcasted_iota(jnp.int32, (TOK, HD), 0)
    low = jnp.full((TOK, HD), CTX * TOK, jnp.int32)
    high = jnp.zeros((TOK, HD), jnp.int32)
    end = jnp.int32(0)
    for i in range(NDOC):
        low = jnp.where(lane == i, end, low)
        end = end + docs[i]
        high = jnp.where(lane == i, end, high)

    def member(d):
        place = lax.rem(ctx + CTX - d, CTX) * TOK + row
        return (place >= low) & (place < high)

    qdoc[...] = jnp.where(member(0), 1.0, 0.0).astype(jnp.bfloat16)

    def mark(d, c):
        kdoc[d] = jnp.where(member(d), 0.0, dead_score).astype(jnp.bfloat16)
        return c

    lax.fori_loop(0, REACH + 1, mark, 0)

    spread = (
        lax.div(lax.broadcasted_iota(jnp.int32, (CTX, TOK), 1), PIECE)
        == lax.broadcasted_iota(jnp.int32, (CTX, TOK), 0)
    ).astype(jnp.bfloat16)
    owners = jnp.broadcast_to(owner[...].astype(jnp.float32), (8, CTX)).astype(jnp.bfloat16)
    owner_of = jnp.dot(owners, spread, preferred_element_type=jnp.float32).astype(jnp.int32)
    column = lax.broadcasted_iota(jnp.int32, (8, TOK), 1)
    goal = (owner_of * PIECE + lax.rem(column, PIECE))[:1]
    swap[...] = (lax.broadcasted_iota(jnp.int32, (TOK, TOK), 0) == goal).astype(jnp.bfloat16)

    own[2].wait()
    for o in range(1, HEADS):
        q_copy(o, source(o), head).wait_recv()

    eye = (
        lax.broadcasted_iota(jnp.int32, (HD, HD), 0) == lax.broadcasted_iota(jnp.int32, (HD, HD), 1)
    ).astype(jnp.bfloat16)
    ones = jnp.ones((EXTRA, WIDE), jnp.bfloat16)

    def across(a, b):
        return lax.dot_general(a, b, (((1,), (1,)), ((), ())), preferred_element_type=jnp.float32)

    for j in range(QPK):
        qt[j, :HD] = across(eye, qbuf[:, j * HD : (j + 1) * HD]).astype(jnp.bfloat16)
        qt[j, HD:] = across(eye, qdoc[...]).astype(jnp.bfloat16)

    def attend(k_rows, k_docs, v_rows, tiles=range(TOK // ROWS), causal=False, fresh=False):
        k_all = jnp.concatenate([k_rows, k_docs], axis=1)
        v_all = jnp.concatenate([across(eye, v_rows).astype(jnp.bfloat16), ones], axis=0)

        def score(j, t):
            rows = slice(t * ROWS, (t + 1) * ROWS)
            s = jnp.dot(k_all, qt[j, :, rows], preferred_element_type=jnp.float32)
            if causal:
                key = lax.broadcasted_iota(jnp.int32, (WIDE, ROWS), 0)
                query = lax.broadcasted_iota(jnp.int32, (WIDE, ROWS), 1)
                s = jnp.where(key <= query, s, dead_score)
            return s

        def weigh(j, t, s):
            rows = slice(t * ROWS, (t + 1) * ROWS)
            peak = jnp.max(s, axis=0, keepdims=True)
            if fresh:
                new, keep = peak, None
            else:
                old = top[j, :1, rows]
                new = jnp.maximum(old, peak)
                keep = jnp.exp2((old - new) * FACTOR)
            top[j, :1, rows] = new
            return jnp.exp2((s - new) * FACTOR).astype(jnp.bfloat16), keep

        def gather(j, t, p, keep):
            rows = slice(t * ROWS, (t + 1) * ROWS)
            pv = jnp.dot(v_all, p, preferred_element_type=jnp.float32)
            if keep is not None:
                pv = pv + acc[j, :, rows] * keep
            acc[j, :, rows] = pv

        order = [(j, t) for j in range(QPK) for t in tiles]
        ss = {0: score(*order[0])}
        pp = {}
        for i in range(len(order) + 1):
            if i + 1 < len(order):
                ss[i + 1] = score(*order[i + 1])
            if i > 0:
                gather(*order[i - 1], *pp[i - 1])
            if i < len(order):
                pp[i] = weigh(*order[i], ss[i])

    def block(begin):
        rows = slice(begin, begin + WIDE)
        return kv[0, 0, rows], kdoc[0, rows], kv[0, 1, rows]

    attend(*block(0), tiles=(0,), causal=True, fresh=True)
    attend(*block(0), tiles=(1,), fresh=True)
    attend(*block(WIDE), tiles=(1,), causal=True)

    def arrive(u):
        for i in range(CHUNKS // 2):
            n = u * (CHUNKS // 2) + i
            ring_copy(n).wait_recv()

            @pl.when(n < (REACH - 1) * CHUNKS)
            def _():
                ring_copy(n + CHUNKS).start()

    def unit(u):
        d = lax.div(u, 2) + 1
        rows = pl.ds(pl.multiple_of(lax.rem(u, 2) * WIDE, WIDE), WIDE)
        attend(kv[d, 0, rows], kdoc[d, rows], kv[d, 1, rows])

    arrive(0)

    def step(u, c):
        arrive(u)
        pl.when(u <= Z // 2)(greet)
        unit(u - 1)
        return c

    lax.fori_loop(1, 2 * REACH, step, 0)
    unit(2 * REACH - 1)

    for j in range(QPK):
        att[j * HD : (j + 1) * HD] = (acc[j, :HD] / acc[j, HD : HD + 1]).astype(jnp.bfloat16)
    ordered[...] = (
        across(swap[...], att[...]).reshape(CTX, PIECE, QPK * HD).astype(jnp.bfloat16)
    )

    def deliver(o, c):
        k = lax.div(o, Y)
        size = Z // 2 - lax.div(k + 1, 2)
        dz = jnp.where(lax.rem(k, 2) == 1, size, Z - size)
        target = at(Y - 1 - lax.rem(o, Y), dz)
        pltpu.make_async_remote_copy(
            src_ref=ordered.at[target],
            dst_ref=out.at[ctx],
            send_sem=out_send,
            recv_sem=out_recv,
            device_id=(target, head),
            device_id_type=MESH,
        ).start()
        return c

    lax.fori_loop(0, CTX - 1, deliver, 0)
    mine = pltpu.make_async_copy(ordered.at[ctx], out.at[ctx], local.at[3])
    mine.start()

    for side in range(2):
        for o in range(1, HEADS):
            kv_copy(o, side, head, peer(o)).wait_send()
    for o in range(1, HEADS):
        q_copy(o, head, peer(o)).wait_send()

    def drain(n, c):
        ring_copy(n).wait_send()
        return c

    lax.fori_loop(0, REACH * CHUNKS, drain, 0)
    mine.wait()
    rest = pltpu.make_async_remote_copy(
        src_ref=ordered.at[pl.ds(0, CTX - 1)],
        dst_ref=out.at[pl.ds(0, CTX - 1)],
        send_sem=out_send,
        recv_sem=out_recv,
        device_id=(following, head),
        device_id_type=MESH,
    )
    rest.wait_send()
    rest.wait_recv()


def per_device(queries, keys, values, doc_lengths, piece_owner):
    whole = pl.BlockSpec(memory_space=pltpu.HBM)
    dma = pltpu.SemaphoreType.DMA
    owned = pl.pallas_call(
        kernel,
        out_shape=jax.ShapeDtypeStruct((CTX, PIECE, QPK * HD), jnp.bfloat16),
        in_specs=[
            whole,
            whole,
            whole,
            whole,
            whole,
        ],
        out_specs=pl.BlockSpec(memory_space=pl.ANY),
        scratch_shapes=[
            pltpu.SMEM((NDOC,), jnp.int32),
            pltpu.VMEM((1, CTX), jnp.int32),
            pltpu.VMEM((TOK, QPK * HD), jnp.bfloat16),
            pltpu.VMEM((REACH + 1, 2, TOK, HD), jnp.bfloat16),
            pltpu.VMEM((TOK, HD), jnp.bfloat16),
            pltpu.VMEM((QPK, 2 * HD, TOK), jnp.bfloat16),
            pltpu.VMEM((REACH + 1, TOK, HD), jnp.bfloat16),
            pltpu.VMEM((QPK, 8, TOK), jnp.float32),
            pltpu.VMEM((QPK, HD + EXTRA, TOK), jnp.float32),
            pltpu.VMEM((QPK * HD, TOK), jnp.bfloat16),
            pltpu.VMEM((TOK, TOK), jnp.bfloat16),
            pltpu.VMEM((CTX, PIECE, QPK * HD), jnp.bfloat16),
            dma((HEADS,)),
            dma((HEADS,)),
            dma((HEADS, 2)),
            dma((HEADS, 2)),
            dma((REACH * CHUNKS,)),
            dma((REACH * CHUNKS,)),
            dma,
            dma,
            dma((6,)),
            pltpu.SemaphoreType.REGULAR,
            pltpu.SemaphoreType.REGULAR,
        ],
        compiler_params=pltpu.CompilerParams(
            collective_id=0, has_side_effects=True, vmem_limit_bytes=66_000_000
        ),
    )(queries, keys, values, doc_lengths, piece_owner)
    return owned.reshape(TOK, QPK * HD)


def solution(mesh):
    return jax.shard_map(
        per_device,
        mesh=mesh,
        in_specs=(
            P(("ctx", "head"), None),
            P(("ctx", "head"), None),
            P(("ctx", "head"), None),
            P(),
            P("ctx", None),
        ),
        out_specs=P("ctx", "head"),
        check_vma=False,
    )
```

```python
import math

import jax
import jax.numpy as jnp
from jax import lax
from jax.experimental import pallas as pl
from jax.experimental.pallas import tpu as pltpu
from jax.sharding import PartitionSpec as P

HD = 128
QPK = 4
MOST = 4096
NDOC = 16
Y = 4
Z = 16
CTX = Y * Z
HEADS = 8
HALF = HEADS // 2
TOK = 512
OWN = TOK // HEADS
REACH = MOST // TOK
PIECE = TOK // CTX
ROWS = 256
EXTRA = 16
WIDE = 256
MESH = pl.DeviceIdType.MESH
dead_score = -1e30
FACTOR = math.log2(math.e) / math.sqrt(HD)


def kernel(
    q_ref,
    k_ref,
    v_ref,
    docs_ref,
    owner_ref,
    out,
    docs,
    owner,
    qbuf,
    kv,
    qdoc,
    qt,
    kdoc,
    top,
    acc,
    att,
    swap,
    ordered,
    q_send,
    q_recv,
    kv_send,
    kv_recv,
    ring_send,
    ring_recv,
    out_send,
    out_recv,
    local,
    from_left,
    from_right,
):
    ctx = lax.axis_index("ctx")
    head = lax.axis_index("head")
    cy, cz = lax.div(ctx, Z), lax.rem(ctx, Z)

    def at(dy, dz):
        return lax.rem(cy + dy, Y) * Z + lax.rem(cz + dz, Z)

    tables = [
        pltpu.make_async_copy(docs_ref, docs, local.at[4]),
        pltpu.make_async_copy(owner_ref, owner, local.at[5]),
    ]
    for copy in tables:
        copy.start()
    following, previous = lax.rem(ctx + 1, CTX), lax.rem(ctx + CTX - 1, CTX)
    left, right = at(0, Z - 1), at(0, 1)
    barrier = pltpu.get_barrier_semaphore()

    def signal(sem, where):
        pl.semaphore_signal(sem, inc=1, device_id=where, device_id_type=MESH)

    for o in range(1, HEADS):
        signal(barrier, (ctx, lax.rem(head + o, HEADS)))
    near = (following, previous, left, right, at(1, 0), at(2, 0), at(3, 0))
    for place in near:
        signal(barrier, (place, head))
    pl.semaphore_wait(barrier, HEADS - 1 + len(near))

    def cols(h, n):
        return pl.ds(pl.multiple_of(h * n, n), n)

    def rows_of(h):
        return pl.ds(pl.multiple_of(h * OWN, OWN), OWN)

    sides = (k_ref, v_ref)

    def kv_copy(o, side, source, target):
        return pltpu.make_async_remote_copy(
            src_ref=sides[side].at[:, cols(target, HD)],
            dst_ref=kv.at[0, side, rows_of(source)],
            send_sem=kv_send.at[o, side],
            recv_sem=kv_recv.at[o, side],
            device_id=(ctx, target),
            device_id_type=MESH,
        )

    def q_copy(o, source, target):
        return pltpu.make_async_remote_copy(
            src_ref=q_ref.at[:, cols(target, QPK * HD)],
            dst_ref=qbuf.at[rows_of(source)],
            send_sem=q_send.at[o],
            recv_sem=q_recv.at[o],
            device_id=(ctx, target),
            device_id_type=MESH,
        )

    half, place_in = lax.div(head, HALF), lax.rem(head, HALF)

    def other(i, step):
        side = half if i < HALF else 1 - half
        return side * HALF + lax.rem(place_in + HALF + step * (i % HALF), HALF)

    def peer(i):
        return other(i, 1)

    def source(i):
        return other(i, -1)

    for o in range(1, HEADS):
        for side in range(2):
            kv_copy(o, side, head, peer(o)).start()
    for o in range(1, HEADS):
        q_copy(o, head, peer(o)).start()
    own = [
        pltpu.make_async_copy(
            sides[side].at[:, cols(head, HD)], kv.at[0, side, rows_of(head)], local.at[side]
        )
        for side in range(2)
    ]
    own.append(
        pltpu.make_async_copy(
            q_ref.at[:, cols(head, QPK * HD)], qbuf.at[rows_of(head)], local.at[2]
        )
    )
    for copy in own:
        copy.start()

    def greet():
        signal(from_left, (right, head))
        signal(from_right, (left, head))
        pl.semaphore_wait(from_left, 1)
        pl.semaphore_wait(from_right, 1)

    def ring_copy(d, i):
        rows = rows_of(source(i))
        return pltpu.make_async_remote_copy(
            src_ref=kv.at[d - 1, :, rows],
            dst_ref=kv.at[d, :, rows],
            send_sem=ring_send.at[d - 1, i],
            recv_sem=ring_recv.at[d - 1, i],
            device_id=(following, head),
            device_id_type=MESH,
        )

    for i in range(HEADS):
        for side in range(2):
            if i == 0:
                own[side].wait()
            else:
                kv_copy(i, side, source(i), head).wait_recv()
        ring_copy(1, i).start()

    def arrive(u):
        d = lax.div(u, 2) + 1
        for i in range(HEADS):

            @pl.when(lax.rem(u, 2) == i // HALF)
            def _():
                ring_copy(d, i).wait_recv()
                pl.when(d < REACH)(ring_copy(d + 1, i).start)

    for copy in tables:
        copy.wait()
    lane = lax.broadcasted_iota(jnp.int32, (TOK, HD), 1)
    row = lax.broadcasted_iota(jnp.int32, (TOK, HD), 0)
    low = jnp.full((TOK, HD), CTX * TOK, jnp.int32)
    high = jnp.zeros((TOK, HD), jnp.int32)
    end = jnp.int32(0)
    for i in range(NDOC):
        low = jnp.where(lane == i, end, low)
        end = end + docs[i]
        high = jnp.where(lane == i, end, high)

    def member(d):
        place = lax.rem(ctx + CTX - d, CTX) * TOK + row
        return (place >= low) & (place < high)

    qdoc[...] = jnp.where(member(0), 1.0, 0.0).astype(jnp.bfloat16)

    def mark(d, c):
        kdoc[d] = jnp.where(member(d), 0.0, dead_score).astype(jnp.bfloat16)
        return c

    lax.fori_loop(0, REACH + 1, mark, 0)

    spread = (
        lax.div(lax.broadcasted_iota(jnp.int32, (CTX, TOK), 1), PIECE)
        == lax.broadcasted_iota(jnp.int32, (CTX, TOK), 0)
    ).astype(jnp.bfloat16)
    owners = jnp.broadcast_to(owner[...].astype(jnp.float32), (8, CTX)).astype(jnp.bfloat16)
    owner_of = jnp.dot(owners, spread, preferred_element_type=jnp.float32).astype(jnp.int32)
    column = lax.broadcasted_iota(jnp.int32, (8, TOK), 1)
    goal = (owner_of * PIECE + lax.rem(column, PIECE))[:1]
    swap[...] = (lax.broadcasted_iota(jnp.int32, (TOK, TOK), 0) == goal).astype(jnp.bfloat16)

    for u in range(3):
        arrive(jnp.int32(u))
    own[2].wait()
    for o in range(1, HEADS):
        q_copy(o, source(o), head).wait_recv()

    eye = (
        lax.broadcasted_iota(jnp.int32, (HD, HD), 0) == lax.broadcasted_iota(jnp.int32, (HD, HD), 1)
    ).astype(jnp.bfloat16)
    ones = jnp.ones((EXTRA, WIDE), jnp.bfloat16)

    def across(a, b):
        return lax.dot_general(a, b, (((1,), (1,)), ((), ())), preferred_element_type=jnp.float32)

    for j in range(QPK):
        qt[j, :HD] = across(eye, qbuf[:, j * HD : (j + 1) * HD]).astype(jnp.bfloat16)
        qt[j, HD:] = across(eye, qdoc[...]).astype(jnp.bfloat16)

    def attend(k_rows, k_docs, v_rows, tiles=range(TOK // ROWS), causal=False, fresh=False):
        k_all = jnp.concatenate([k_rows, k_docs], axis=1)
        v_all = jnp.concatenate([across(eye, v_rows).astype(jnp.bfloat16), ones], axis=0)

        def score(j, t):
            rows = slice(t * ROWS, (t + 1) * ROWS)
            s = jnp.dot(k_all, qt[j, :, rows], preferred_element_type=jnp.float32)
            if causal:
                key = lax.broadcasted_iota(jnp.int32, (WIDE, ROWS), 0)
                query = lax.broadcasted_iota(jnp.int32, (WIDE, ROWS), 1)
                s = jnp.where(key <= query, s, dead_score)
            return s

        def weigh(j, t, s):
            rows = slice(t * ROWS, (t + 1) * ROWS)
            peak = jnp.max(s, axis=0, keepdims=True)
            if fresh:
                new, keep = peak, None
            else:
                old = top[j, :1, rows]
                new = jnp.maximum(old, peak)
                keep = jnp.exp2((old - new) * FACTOR)
            top[j, :1, rows] = new
            return jnp.exp2((s - new) * FACTOR).astype(jnp.bfloat16), keep

        def gather(j, t, p, keep):
            rows = slice(t * ROWS, (t + 1) * ROWS)
            pv = jnp.dot(v_all, p, preferred_element_type=jnp.float32)
            if keep is not None:
                pv = pv + acc[j, :, rows] * keep
            acc[j, :, rows] = pv

        order = [(j, t) for j in range(QPK) for t in tiles]
        ss = {0: score(*order[0])}
        pp = {}
        for i in range(len(order) + 1):
            if i + 1 < len(order):
                ss[i + 1] = score(*order[i + 1])
            if i > 0:
                gather(*order[i - 1], *pp[i - 1])
            if i < len(order):
                pp[i] = weigh(*order[i], ss[i])

    def block(begin):
        rows = slice(begin, begin + WIDE)
        return kv[0, 0, rows], kdoc[0, rows], kv[0, 1, rows]

    attend(*block(0), tiles=(0,), causal=True, fresh=True)
    attend(*block(0), tiles=(1,), fresh=True)
    attend(*block(WIDE), tiles=(1,), causal=True)

    def unit(u, c=0):
        d = lax.div(u, 2) + 1
        side = jnp.where(lax.rem(u, 2) == 0, half, 1 - half)
        rows = pl.ds(pl.multiple_of(side * WIDE, WIDE), WIDE)
        attend(kv[d, 0, rows], kdoc[d, rows], kv[d, 1, rows])
        return c

    arrive(jnp.int32(3))
    for u, units in ((4, (0, 2)), (5, (2, 4)), (6, (4, 5)), (7, (5, 7))):
        arrive(jnp.int32(u))
        lax.fori_loop(*units, unit, 0)

    def step(u, c):
        arrive(u)
        greet()
        return unit(u - 1, c)

    lax.fori_loop(Z // 2, 2 * REACH, step, 0)
    unit(jnp.int32(2 * REACH - 1))

    for j in range(QPK):
        att[j * HD : (j + 1) * HD] = (acc[j, :HD] / acc[j, HD : HD + 1]).astype(jnp.bfloat16)
    ordered[...] = (
        across(swap[...], att[...]).reshape(CTX, PIECE, QPK * HD).astype(jnp.bfloat16)
    )

    def deliver(o, c):
        k = lax.div(o, Y)
        size = Z // 2 - lax.div(k + 1, 2)
        dz = jnp.where(lax.rem(k, 2) == 1, size, Z - size)
        target = at(Y - 1 - lax.rem(o, Y), dz)
        pltpu.make_async_remote_copy(
            src_ref=ordered.at[target],
            dst_ref=out.at[ctx],
            send_sem=out_send,
            recv_sem=out_recv,
            device_id=(target, head),
            device_id_type=MESH,
        ).start()
        return c

    lax.fori_loop(0, CTX - 1, deliver, 0)
    mine = pltpu.make_async_copy(ordered.at[ctx], out.at[ctx], local.at[3])
    mine.start()

    for side in range(2):
        for o in range(1, HEADS):
            kv_copy(o, side, head, peer(o)).wait_send()
    for o in range(1, HEADS):
        q_copy(o, head, peer(o)).wait_send()

    def drain(d, c):
        for i in range(HEADS):
            ring_copy(d, i).wait_send()
        return c

    lax.fori_loop(1, REACH + 1, drain, 0)
    mine.wait()
    rest = pltpu.make_async_remote_copy(
        src_ref=ordered.at[pl.ds(0, CTX - 1)],
        dst_ref=out.at[pl.ds(0, CTX - 1)],
        send_sem=out_send,
        recv_sem=out_recv,
        device_id=(following, head),
        device_id_type=MESH,
    )
    rest.wait_send()
    rest.wait_recv()


def per_device(queries, keys, values, doc_lengths, piece_owner):
    whole = pl.BlockSpec(memory_space=pltpu.HBM)
    dma = pltpu.SemaphoreType.DMA
    owned = pl.pallas_call(
        kernel,
        out_shape=jax.ShapeDtypeStruct((CTX, PIECE, QPK * HD), jnp.bfloat16),
        in_specs=[
            whole,
            whole,
            whole,
            whole,
            whole,
        ],
        out_specs=pl.BlockSpec(memory_space=pl.ANY),
        scratch_shapes=[
            pltpu.SMEM((NDOC,), jnp.int32),
            pltpu.VMEM((1, CTX), jnp.int32),
            pltpu.VMEM((TOK, QPK * HD), jnp.bfloat16),
            pltpu.VMEM((REACH + 1, 2, TOK, HD), jnp.bfloat16),
            pltpu.VMEM((TOK, HD), jnp.bfloat16),
            pltpu.VMEM((QPK, 2 * HD, TOK), jnp.bfloat16),
            pltpu.VMEM((REACH + 1, TOK, HD), jnp.bfloat16),
            pltpu.VMEM((QPK, 8, TOK), jnp.float32),
            pltpu.VMEM((QPK, HD + EXTRA, TOK), jnp.float32),
            pltpu.VMEM((QPK * HD, TOK), jnp.bfloat16),
            pltpu.VMEM((TOK, TOK), jnp.bfloat16),
            pltpu.VMEM((CTX, PIECE, QPK * HD), jnp.bfloat16),
            dma((HEADS,)),
            dma((HEADS,)),
            dma((HEADS, 2)),
            dma((HEADS, 2)),
            dma((REACH, HEADS)),
            dma((REACH, HEADS)),
            dma,
            dma,
            dma((6,)),
            pltpu.SemaphoreType.REGULAR,
            pltpu.SemaphoreType.REGULAR,
        ],
        compiler_params=pltpu.CompilerParams(
            collective_id=0, has_side_effects=True, vmem_limit_bytes=66_000_000
        ),
    )(queries, keys, values, doc_lengths, piece_owner)
    return owned.reshape(TOK, QPK * HD)


def solution(mesh):
    return jax.shard_map(
        per_device,
        mesh=mesh,
        in_specs=(
            P(("ctx", "head"), None),
            P(("ctx", "head"), None),
            P(("ctx", "head"), None),
            P(),
            P("ctx", None),
        ),
        out_specs=P("ctx", "head"),
        check_vma=False,
    )
```

```python
import math

import jax
import jax.numpy as jnp
from jax import lax
from jax.experimental import pallas as pl
from jax.experimental.pallas import tpu as pltpu
from jax.sharding import PartitionSpec as P

HD = 128
QPK = 4
MOST = 4096
NDOC = 16
Y = 4
Z = 16
CTX = Y * Z
HEADS = 8
HALF = HEADS // 2
TOK = 512
OWN = TOK // HEADS
REACH = MOST // TOK
PIECE = TOK // CTX
ROWS = 256
EXTRA = 16
WIDE = 256
MESH = pl.DeviceIdType.MESH
dead_score = -1e30
FACTOR = math.log2(math.e) / math.sqrt(HD)


def kernel(
    q_ref,
    k_ref,
    v_ref,
    docs_ref,
    owner_ref,
    out,
    docs,
    owner,
    qbuf,
    kv,
    qdoc,
    qt,
    kdoc,
    top,
    acc,
    att,
    swap,
    ordered,
    q_send,
    q_recv,
    kv_send,
    kv_recv,
    ring_send,
    ring_recv,
    out_send,
    out_recv,
    local,
    from_left,
    from_right,
):
    ctx = lax.axis_index("ctx")
    head = lax.axis_index("head")
    cy, cz = lax.div(ctx, Z), lax.rem(ctx, Z)

    def at(dy, dz):
        return lax.rem(cy + dy, Y) * Z + lax.rem(cz + dz, Z)

    tables = [
        pltpu.make_async_copy(docs_ref, docs, local.at[4]),
        pltpu.make_async_copy(owner_ref, owner, local.at[5]),
    ]
    for copy in tables:
        copy.start()
    following, previous = lax.rem(ctx + 1, CTX), lax.rem(ctx + CTX - 1, CTX)
    left, right = at(0, Z - 1), at(0, 1)
    barrier = pltpu.get_barrier_semaphore()

    def signal(sem, where):
        pl.semaphore_signal(sem, inc=1, device_id=where, device_id_type=MESH)

    for o in range(1, HEADS):
        signal(barrier, (ctx, lax.rem(head + o, HEADS)))
    near = (following, previous, left, right, at(1, 0), at(2, 0), at(3, 0))
    for place in near:
        signal(barrier, (place, head))
    pl.semaphore_wait(barrier, HEADS - 1 + len(near))

    def cols(h, n):
        return pl.ds(pl.multiple_of(h * n, n), n)

    def rows_of(h):
        return pl.ds(pl.multiple_of(h * OWN, OWN), OWN)

    sides = (k_ref, v_ref)

    def kv_copy(o, side, source, target):
        return pltpu.make_async_remote_copy(
            src_ref=sides[side].at[:, cols(target, HD)],
            dst_ref=kv.at[0, side, rows_of(source)],
            send_sem=kv_send.at[o, side],
            recv_sem=kv_recv.at[o, side],
            device_id=(ctx, target),
            device_id_type=MESH,
        )

    def q_copy(o, source, target):
        return pltpu.make_async_remote_copy(
            src_ref=q_ref.at[:, cols(target, QPK * HD)],
            dst_ref=qbuf.at[rows_of(source)],
            send_sem=q_send.at[o],
            recv_sem=q_recv.at[o],
            device_id=(ctx, target),
            device_id_type=MESH,
        )

    half, place_in = lax.div(head, HALF), lax.rem(head, HALF)

    def other(i, step):
        side = half if i < HALF else 1 - half
        return side * HALF + lax.rem(place_in + HALF + step * (i % HALF), HALF)

    def peer(i):
        return other(i, 1)

    def source(i):
        return other(i, -1)

    for o in range(1, HEADS):
        for side in range(2):
            kv_copy(o, side, head, peer(o)).start()
    for o in range(1, HEADS):
        q_copy(o, head, peer(o)).start()
    own = [
        pltpu.make_async_copy(
            sides[side].at[:, cols(head, HD)], kv.at[0, side, rows_of(head)], local.at[side]
        )
        for side in range(2)
    ]
    own.append(
        pltpu.make_async_copy(
            q_ref.at[:, cols(head, QPK * HD)], qbuf.at[rows_of(head)], local.at[2]
        )
    )
    for copy in own:
        copy.start()

    def greet():
        signal(from_left, (right, head))
        signal(from_right, (left, head))
        pl.semaphore_wait(from_left, 1)
        pl.semaphore_wait(from_right, 1)

    def ring_copy(d, i):
        rows = rows_of(source(i))
        return pltpu.make_async_remote_copy(
            src_ref=kv.at[d - 1, :, rows],
            dst_ref=kv.at[d, :, rows],
            send_sem=ring_send.at[d - 1, i],
            recv_sem=ring_recv.at[d - 1, i],
            device_id=(following, head),
            device_id_type=MESH,
        )

    for i in range(HEADS):
        for side in range(2):
            if i == 0:
                own[side].wait()
            else:
                kv_copy(i, side, source(i), head).wait_recv()
        ring_copy(1, i).start()

    def arrive(u):
        d = lax.div(u, 2) + 1
        for i in range(HEADS):

            @pl.when(lax.rem(u, 2) == i // HALF)
            def _():
                ring_copy(d, i).wait_recv()
                pl.when(d < REACH)(ring_copy(d + 1, i).start)

    for copy in tables:
        copy.wait()
    lane = lax.broadcasted_iota(jnp.int32, (TOK, HD), 1)
    row = lax.broadcasted_iota(jnp.int32, (TOK, HD), 0)
    low = jnp.full((TOK, HD), CTX * TOK, jnp.int32)
    high = jnp.zeros((TOK, HD), jnp.int32)
    end = jnp.int32(0)
    for i in range(NDOC):
        low = jnp.where(lane == i, end, low)
        end = end + docs[i]
        high = jnp.where(lane == i, end, high)

    def member(d):
        place = lax.rem(ctx + CTX - d, CTX) * TOK + row
        return (place >= low) & (place < high)

    qdoc[...] = jnp.where(member(0), 1.0, 0.0).astype(jnp.bfloat16)

    def mark(d, c):
        kdoc[d] = jnp.where(member(d), 0.0, dead_score).astype(jnp.bfloat16)
        return c

    lax.fori_loop(0, REACH + 1, mark, 0)

    spread = (
        lax.div(lax.broadcasted_iota(jnp.int32, (CTX, TOK), 1), PIECE)
        == lax.broadcasted_iota(jnp.int32, (CTX, TOK), 0)
    ).astype(jnp.bfloat16)
    owners = jnp.broadcast_to(owner[...].astype(jnp.float32), (8, CTX)).astype(jnp.bfloat16)
    owner_of = jnp.dot(owners, spread, preferred_element_type=jnp.float32).astype(jnp.int32)
    column = lax.broadcasted_iota(jnp.int32, (8, TOK), 1)
    goal = (owner_of * PIECE + lax.rem(column, PIECE))[:1]
    swap[...] = (lax.broadcasted_iota(jnp.int32, (TOK, TOK), 0) == goal).astype(jnp.bfloat16)

    for u in range(3):
        arrive(jnp.int32(u))
    own[2].wait()
    for o in range(1, HEADS):
        q_copy(o, source(o), head).wait_recv()

    eye = (
        lax.broadcasted_iota(jnp.int32, (HD, HD), 0) == lax.broadcasted_iota(jnp.int32, (HD, HD), 1)
    ).astype(jnp.bfloat16)
    ones = jnp.ones((EXTRA, WIDE), jnp.bfloat16)

    def across(a, b):
        return lax.dot_general(a, b, (((1,), (1,)), ((), ())), preferred_element_type=jnp.float32)

    for j in range(QPK):
        qt[j, :HD] = across(eye, qbuf[:, j * HD : (j + 1) * HD]).astype(jnp.bfloat16)
        qt[j, HD:] = across(eye, qdoc[...]).astype(jnp.bfloat16)

    def attend(k_rows, k_docs, v_rows, tiles=range(TOK // ROWS), causal=False, fresh=False):
        k_all = jnp.concatenate([k_rows, k_docs], axis=1)
        v_all = jnp.concatenate([across(eye, v_rows).astype(jnp.bfloat16), ones], axis=0)

        def score(j, t):
            rows = slice(t * ROWS, (t + 1) * ROWS)
            s = jnp.dot(k_all, qt[j, :, rows], preferred_element_type=jnp.float32)
            if causal:
                key = lax.broadcasted_iota(jnp.int32, (WIDE, ROWS), 0)
                query = lax.broadcasted_iota(jnp.int32, (WIDE, ROWS), 1)
                s = jnp.where(key <= query, s, dead_score)
            return s

        def weigh(j, t, s):
            rows = slice(t * ROWS, (t + 1) * ROWS)
            peak = jnp.max(s, axis=0, keepdims=True)
            if fresh:
                new, keep = peak, None
            else:
                old = top[j, :1, rows]
                new = jnp.maximum(old, peak)
                keep = jnp.exp2((old - new) * FACTOR)
            top[j, :1, rows] = new
            return jnp.exp2((s - new) * FACTOR).astype(jnp.bfloat16), keep

        def gather(j, t, p, keep):
            rows = slice(t * ROWS, (t + 1) * ROWS)
            pv = jnp.dot(v_all, p, preferred_element_type=jnp.float32)
            if keep is not None:
                pv = pv + acc[j, :, rows] * keep
            acc[j, :, rows] = pv

        order = [(j, t) for j in range(QPK) for t in tiles]
        ss = {0: score(*order[0])}
        pp = {}
        for i in range(len(order) + 1):
            if i + 1 < len(order):
                ss[i + 1] = score(*order[i + 1])
            if i > 0:
                gather(*order[i - 1], *pp[i - 1])
            if i < len(order):
                pp[i] = weigh(*order[i], ss[i])

    def block(begin):
        rows = slice(begin, begin + WIDE)
        return kv[0, 0, rows], kdoc[0, rows], kv[0, 1, rows]

    attend(*block(0), tiles=(0,), causal=True, fresh=True)
    attend(*block(0), tiles=(1,), fresh=True)
    attend(*block(WIDE), tiles=(1,), causal=True)

    def unit(u, c=0):
        d = lax.div(u, 2) + 1
        side = jnp.where(lax.rem(u, 2) == 0, half, 1 - half)
        rows = pl.ds(pl.multiple_of(side * WIDE, WIDE), WIDE)
        attend(kv[d, 0, rows], kdoc[d, rows], kv[d, 1, rows])
        return c

    arrive(jnp.int32(3))
    for u, units in ((4, (0, 2)), (5, (2, 4)), (6, (4, 5)), (7, (5, 7))):
        arrive(jnp.int32(u))
        lax.fori_loop(*units, unit, 0)

    def step(u, c):
        arrive(u)
        greet()
        return unit(u - 1, c)

    lax.fori_loop(Z // 2, 2 * REACH, step, 0)
    unit(jnp.int32(2 * REACH - 1))

    for j in range(QPK):
        att[j * HD : (j + 1) * HD] = (acc[j, :HD] / acc[j, HD : HD + 1]).astype(jnp.bfloat16)
    ordered[...] = (
        across(swap[...], att[...]).reshape(CTX, PIECE, QPK * HD).astype(jnp.bfloat16)
    )

    def deliver(o, c):
        k = lax.rem(o, Z)
        size = Z // 2 - lax.div(k + 1, 2)
        dz = jnp.where(lax.rem(k, 2) == 1, size, Z - size)
        target = at(Y - 1 - lax.div(o, Z), dz)
        pltpu.make_async_remote_copy(
            src_ref=ordered.at[target],
            dst_ref=out.at[ctx],
            send_sem=out_send,
            recv_sem=out_recv,
            device_id=(target, head),
            device_id_type=MESH,
        ).start()
        return c

    lax.fori_loop(0, CTX - 1, deliver, 0)
    mine = pltpu.make_async_copy(ordered.at[ctx], out.at[ctx], local.at[3])
    mine.start()

    for side in range(2):
        for o in range(1, HEADS):
            kv_copy(o, side, head, peer(o)).wait_send()
    for o in range(1, HEADS):
        q_copy(o, head, peer(o)).wait_send()

    def drain(d, c):
        for i in range(HEADS):
            ring_copy(d, i).wait_send()
        return c

    lax.fori_loop(1, REACH + 1, drain, 0)
    mine.wait()
    rest = pltpu.make_async_remote_copy(
        src_ref=ordered.at[pl.ds(0, CTX - 1)],
        dst_ref=out.at[pl.ds(0, CTX - 1)],
        send_sem=out_send,
        recv_sem=out_recv,
        device_id=(following, head),
        device_id_type=MESH,
    )
    rest.wait_send()
    rest.wait_recv()


def per_device(queries, keys, values, doc_lengths, piece_owner):
    whole = pl.BlockSpec(memory_space=pltpu.HBM)
    dma = pltpu.SemaphoreType.DMA
    owned = pl.pallas_call(
        kernel,
        out_shape=jax.ShapeDtypeStruct((CTX, PIECE, QPK * HD), jnp.bfloat16),
        in_specs=[
            whole,
            whole,
            whole,
            whole,
            whole,
        ],
        out_specs=pl.BlockSpec(memory_space=pl.ANY),
        scratch_shapes=[
            pltpu.SMEM((NDOC,), jnp.int32),
            pltpu.VMEM((1, CTX), jnp.int32),
            pltpu.VMEM((TOK, QPK * HD), jnp.bfloat16),
            pltpu.VMEM((REACH + 1, 2, TOK, HD), jnp.bfloat16),
            pltpu.VMEM((TOK, HD), jnp.bfloat16),
            pltpu.VMEM((QPK, 2 * HD, TOK), jnp.bfloat16),
            pltpu.VMEM((REACH + 1, TOK, HD), jnp.bfloat16),
            pltpu.VMEM((QPK, 8, TOK), jnp.float32),
            pltpu.VMEM((QPK, HD + EXTRA, TOK), jnp.float32),
            pltpu.VMEM((QPK * HD, TOK), jnp.bfloat16),
            pltpu.VMEM((TOK, TOK), jnp.bfloat16),
            pltpu.VMEM((CTX, PIECE, QPK * HD), jnp.bfloat16),
            dma((HEADS,)),
            dma((HEADS,)),
            dma((HEADS, 2)),
            dma((HEADS, 2)),
            dma((REACH, HEADS)),
            dma((REACH, HEADS)),
            dma,
            dma,
            dma((6,)),
            pltpu.SemaphoreType.REGULAR,
            pltpu.SemaphoreType.REGULAR,
        ],
        compiler_params=pltpu.CompilerParams(
            collective_id=0, has_side_effects=True, vmem_limit_bytes=66_000_000
        ),
    )(queries, keys, values, doc_lengths, piece_owner)
    return owned.reshape(TOK, QPK * HD)


def solution(mesh):
    return jax.shard_map(
        per_device,
        mesh=mesh,
        in_specs=(
            P(("ctx", "head"), None),
            P(("ctx", "head"), None),
            P(("ctx", "head"), None),
            P(),
            P("ctx", None),
        ),
        out_specs=P("ctx", "head"),
        check_vma=False,
    )
```
